32 devices in a mesh: expert: 8 (over z, x), tensor: 4 (over y, core).
Axes of the slice: x: 2, y: 2, z: 4, core: 2. Of those that a mesh axis runs over, the one named last changes fastest.
Arguments:
- hidden_in: bfloat16 [4096, 2048], P('expert'), may hold values from -6 to 6
- doc_ids: int32 [8, 512], P('expert'), may hold values from 0 to 2, never falling along the last dimension, each value on 1 to 384 neighbouring positions
- routes: int32 [4096, 8], P('expert'), may hold values from 0 to 15, all different within a row
- out_grad: bfloat16 [4096, 2048], P('expert'), may hold values from -6 to 6
- norm1_gain: float32 [2048], replicated, may hold values from 0.5 to 1.5
- q_weight: bfloat16 [2048, 2048], P(None, 'tensor'), may hold values from -0.125 to 0.125
- k_weight: bfloat16 [2048, 2048], P(None, 'tensor'), may hold values from -0.125 to 0.125
- v_weight: bfloat16 [2048, 2048], P(None, 'tensor'), may hold values from -0.125 to 0.125
- o_weight: bfloat16 [2048, 2048], P(None, 'tensor'), may hold values from -1.5 to 1.5
- q_gain: float32 [128], replicated, may hold values from 0.5 to 1.5
- k_gain: float32 [128], replicated, may hold values from 0.5 to 1.5
- norm2_gain: float32 [2048], replicated, may hold values from 0.5 to 1.5
- router_weight: bfloat16 [2048, 16], replicated, may hold values from -0.0625 to 0.0625
- gate_weight: bfloat16 [16, 2048, 1024], P('expert', None, 'tensor'), may hold values from -0.125 to 0.125
- up_weight: bfloat16 [16, 2048, 1024], P('expert', None, 'tensor'), may hold values from -0.125 to 0.125
- down_weight: bfloat16 [16, 1024, 2048], P('expert', 'tensor'), may hold values from -0.5 to 0.5
Outputs:
- output: bfloat16 [4096, 2048], P('expert')
- input_grad: float32 [4096, 2048], P('expert')
- norm1_gain_grad: float32 [2048], P('expert')
- q_weight_grad: float32 [2048, 2048], P('expert', 'tensor')
- k_weight_grad: float32 [2048, 2048], P('expert', 'tensor')
- v_weight_grad: float32 [2048, 2048], P('expert', 'tensor')
- o_weight_grad: float32 [2048, 2048], P('expert', 'tensor')
- q_gain_grad: float32 [128], P('expert')
- k_gain_grad: float32 [128], P('expert')
- norm2_gain_grad: float32 [2048], P('expert')
- router_weight_grad: float32 [2048, 16], P('expert')
- gate_weight_grad: float32 [16, 2048, 1024], P('expert', None, 'tensor')
- up_weight_grad: float32 [16, 2048, 1024], P('expert', None, 'tensor')
- down_weight_grad: float32 [16, 1024, 2048], P('expert', 'tensor')
The draws below stay inside these ranges and needn't reach their ends.
Inputs may be any that keep to these rules, and one draw needn't show every extreme that they name: Each row of routes names 8 different experts. `doc_ids`: within a packed row ids never fall; a document has at most 384 tokens.
All inputs are finite; a program needn't handle non-finite values.
Results may differ from the reference program's by a relative error of at most 0.024.
Values may be sent and summed in bfloat16 or wider, within the bound.
No kernel may reach another device: no remote copies, remote signals or barrier semaphores. Data moves between devices by JAX's collectives and lax.ppermute only.
A program may use at most 320 MiB of HBM per device.

```python
import math
import jax
import jax.numpy as jnp
import numpy as np
from jax import lax

D = 2048
HEADS = 16
HEAD_DIM = 128
EXP_FF = 1024
TOPK = 8
TOK_DEV = 512
EXPERTS = 16
GROUPS = 8
TOKENS = 4096
CAP = 288
DOC_MOST = 384
QB = 512
N_TENSOR = 4


def level_of(key, dims, cuts, least, largest):
    loudness, own = 1.0, jax.random.fold_in(key, 6)
    for position, parts in cuts:
        heights = jnp.exp(jax.random.uniform(jax.random.fold_in(own, position), (parts,), jnp.float32, least / len(cuts), largest / len(cuts)))
        loudness = loudness * jnp.repeat(heights, dims[position] // parts).reshape([-1 if axis == position else 1 for axis in range(len(dims))])
    return loudness


def picks_of(rng, rows, amount, top, lift):
    ranking = jax.random.permutation(jax.random.fold_in(rng, 1), amount)
    favour = ranking
    for power in range(3):
        favour = favour * favour // amount
    favour = favour * lift // amount
    chance = jax.random.randint(jax.random.fold_in(rng, 2), (rows, amount), 0, 4096) + favour
    holders = jax.random.permutation(jax.random.fold_in(rng, 3), rows)[jnp.arange(amount) % rows]
    chance = jnp.where(jnp.arange(rows)[:, None] == holders[None, :], 1 << 14, chance)
    merit = chance * amount + jnp.arange(amount)
    return lax.top_k(merit.astype(jnp.int32), top)[1].astype(jnp.int32)


def length_profile(number_of, total, bound, lean):
    loads = [(1 << 20) // math.isqrt(grade ** lean) + 1 for grade in range(2, number_of + 1)]
    surplus, given = total - bound - (number_of - 1), [1] * (number_of - 1)
    while surplus > 0:
        movable = [i for i in range(number_of - 1) if given[i] < bound]
        whole, budget = sum([loads[i] for i in movable]), surplus
        for i in movable:
            extra = min(bound - given[i], max(1, budget * loads[i] // whole), surplus)
            given[i] = given[i] + extra
            surplus = surplus - extra
    return np.array([bound] + given)


def uneven(rng, count, total, most, slope):
    if count == 2:
        one = jax.random.randint(rng, (), max(1, total - most), min(most, total - 1) + 1)
        return jnp.stack([one, total - one])
    tallies = jnp.asarray(length_profile(count, total, most, slope), jnp.int32)
    pairs = (count - 1) // 2
    donor, sink = tallies[1:1 + 2 * pairs:2], tallies[2:2 + 2 * pairs:2]
    slack = jnp.minimum(donor - 1, most - sink)
    passed = jax.random.randint(jax.random.fold_in(rng, 1), (pairs,), 0, 1 << 20) % (slack + 1)
    tallies = tallies.at[1:1 + 2 * pairs:2].set(donor - passed).at[2:2 + 2 * pairs:2].set(sink + passed)
    return tallies[jax.random.permutation(jax.random.fold_in(rng, 2), count)]


def bell_draw(own_key, shape, spread, most, shards=(), kind=jnp.bfloat16):
    level = level_of(own_key, shape, shards, -0.22, 0.18) if shards else 1.0
    values = jax.random.normal(own_key, shape, jnp.float32) * spread * level
    return jnp.minimum(jnp.maximum(values, -most), most).astype(kind)


def setup_inputs(seed: int = 0) -> dict:
    streams_of = jax.random.split(jax.random.key(seed), 17)
    return {
        "hidden_in": bell_draw(streams_of[0], (TOKENS, D), 1.0, 6.0, ((0, 8),)),
        "doc_ids": jax.vmap(lambda own: jnp.searchsorted(jnp.cumsum(uneven(own, 3, TOK_DEV, DOC_MOST, 0)), jnp.arange(TOK_DEV), side="right"))(jax.random.split(streams_of[1], GROUPS)).reshape((GROUPS, TOK_DEV)).astype(jnp.int32),
        "routes": picks_of(streams_of[2], TOKENS, EXPERTS, TOPK, 4096),
        "out_grad": bell_draw(streams_of[3], (TOKENS, D), 1.0, 6.0, ((0, 8),)),
        "norm1_gain": jnp.clip(1.0 + 0.1 * jax.random.normal(streams_of[4], (D,), jnp.float32), 0.5, 1.5),
        "q_weight": bell_draw(streams_of[5], (D, HEADS * HEAD_DIM), D ** -0.5, 0.125, ((1, 4),)),
        "k_weight": bell_draw(streams_of[6], (D, HEADS * HEAD_DIM), D ** -0.5, 0.125, ((1, 4),)),
        "v_weight": bell_draw(streams_of[7], (D, HEADS * HEAD_DIM), D ** -0.5, 0.125, ((1, 4),)),
        "o_weight": bell_draw(streams_of[8], (D, HEADS * HEAD_DIM), (HEADS * HEAD_DIM * 4 // TOK_DEV) ** -0.5, 1.5, ((1, 4),)),
        "q_gain": jnp.clip(1.0 + 0.1 * jax.random.normal(streams_of[9], (HEAD_DIM,), jnp.float32), 0.5, 1.5),
        "k_gain": jnp.clip(1.0 + 0.1 * jax.random.normal(streams_of[10], (HEAD_DIM,), jnp.float32), 0.5, 1.5),
        "norm2_gain": jnp.clip(1.0 + 0.1 * jax.random.normal(streams_of[11], (D,), jnp.float32), 0.5, 1.5),
        "router_weight": bell_draw(streams_of[12], (D, EXPERTS), (4 * D) ** -0.5, 0.0625),
        "gate_weight": bell_draw(streams_of[13], (EXPERTS, D, EXP_FF), D ** -0.5, 0.125, ((0, 8), (2, 4))),
        "up_weight": bell_draw(streams_of[14], (EXPERTS, D, EXP_FF), D ** -0.5, 0.125, ((0, 8), (2, 4))),
        "down_weight": bell_draw(streams_of[15], (EXPERTS, EXP_FF, D), (EXP_FF // 8) ** -0.5, 0.5, ((0, 8), (1, 4))),
    }


epsilon = 1e-06
rope_base = 10000.0
masked_score = -1e+30
precise = lax.Precision.HIGHEST

@jax.custom_vjp
def low(v):
    return lax.optimization_barrier(v.astype(jnp.bfloat16)).astype(jnp.float32)

@jax.custom_vjp
def low_back(v):
    return v

def low_keep(v):
    return (low(v), None)

def low_pass(kept, grad):
    return (grad,)

def back_keep(v):
    return (v, None)

def back_low(kept, grad):
    return (low(grad),)
low.defvjp(low_keep, low_pass)
low_back.defvjp(back_keep, back_low)

def rms_scale(values):
    return lax.rsqrt(lax.optimization_barrier(jnp.mean(values * values, axis=-1, keepdims=True)) + epsilon)

def rotary(positions, head_size):
    half_size = head_size // 2
    freqs = rope_base ** (-2.0 * jnp.arange(half_size, dtype=jnp.float32) / head_size)
    angles = jnp.arange(positions, dtype=jnp.float32)[:, None] * freqs[None, :]
    cosine = jnp.cos(angles)
    sine = jnp.sin(angles)
    return (jnp.concatenate([cosine, cosine], -1), jnp.concatenate([sine, sine], -1))

def prep_heads(raw, gain, factor, cosine, sine, heads):
    shaped = raw.reshape(raw.shape[0], heads, -1)
    normed = shaped * rms_scale(shaped) * gain
    half_size = normed.shape[-1] // 2
    turned = jnp.concatenate([-normed[..., half_size:], normed[..., :half_size]], -1)
    return (normed * cosine[:, None, :] + turned * sine[:, None, :]) * factor

def attend_block(query_blk, doc_blk, keys, values, doc_row):
    scores = low_back(jnp.einsum('qhd,khd->hqk', query_blk, keys, precision=precise))
    scores = jnp.where((doc_blk[:, None] == doc_row[None, :])[None], scores, masked_score)
    peak = lax.optimization_barrier(jnp.max(scores, -1, keepdims=True))
    log_total = peak + jnp.log(lax.optimization_barrier(jnp.sum(jnp.exp(scores - peak), -1, keepdims=True)))
    weights = low(jnp.exp(scores - log_total))
    return jnp.einsum('hqk,khd->qhd', weights, values, precision=precise)

def attend_group(group_rows, doc_row, g_one, w_query, w_key, w_value, w_out, q_scale, k_scale):
    positions = group_rows.shape[0]
    cosine, sine = rotary(positions, HEAD_DIM)
    normed = low(group_rows * rms_scale(group_rows) * g_one)
    q_raw = low_back(jnp.dot(normed, w_query, precision=precise))
    k_raw = low_back(jnp.dot(normed, w_key, precision=precise))
    values = low(low_back(jnp.dot(normed, w_value, precision=precise))).reshape(positions, HEADS, HEAD_DIM)
    queries = low(prep_heads(q_raw, q_scale, HEAD_DIM ** (-0.5), cosine, sine, HEADS))
    keys = low(prep_heads(k_raw, k_scale, 1.0, cosine, sine, HEADS))
    blocks = positions // QB
    block_step = jax.checkpoint(attend_block)
    attn_out = lax.map(lambda packed: block_step(packed[0], packed[1], keys, values, doc_row), (queries.reshape(blocks, QB, HEADS, HEAD_DIM), doc_row.reshape(blocks, QB)))
    attn_out = low(low_back(attn_out.reshape(positions, HEADS * HEAD_DIM)))
    branch = low_back(jnp.dot(attn_out, w_out.T, precision=precise))
    return group_rows + branch

def expert_rows(padded, w_gate, w_up, w_down, owner):
    slot_rows = jax.vmap(lambda table, index: jnp.take(table, index, axis=0))(padded, owner)
    quarter_width = EXP_FF // N_TENSOR
    summed = jnp.zeros(slot_rows.shape, jnp.float32)
    for quarter in range(N_TENSOR):
        first_col = quarter * quarter_width
        slot_input = low_back(slot_rows)
        gate_pre = low_back(jnp.einsum('gcd,df->gcf', slot_input, w_gate[:, first_col:first_col + quarter_width], precision=precise))
        up_pre = low_back(jnp.einsum('gcd,df->gcf', slot_input, w_up[:, first_col:first_col + quarter_width], precision=precise))
        hidden = low(jax.nn.silu(gate_pre) * up_pre)
        summed = summed + low(low_back(jnp.einsum('gcf,fd->gcd', hidden, w_down[first_col:first_col + quarter_width], precision=precise)))
    return summed

def slot_tables(route_rows):
    num_tokens, num_picks = route_rows.shape
    flat_routes = route_rows.reshape(-1)
    onehot = (flat_routes[:, None] == jnp.arange(EXPERTS, dtype=jnp.int32)[None, :]).astype(jnp.int32)
    before = jnp.cumsum(onehot, axis=0) - onehot
    placed = lax.optimization_barrier(jnp.sum(before * onehot, axis=1))
    slot_ids = jnp.where(placed < CAP, flat_routes * CAP + placed, EXPERTS * CAP).astype(jnp.int32)
    pair_ids = jnp.arange(num_tokens * num_picks, dtype=jnp.int32)
    owners = jnp.full((EXPERTS * CAP + 1,), num_tokens, jnp.int32).at[slot_ids].set(pair_ids // num_picks)
    return (slot_ids.reshape(num_tokens, num_picks), owners[:-1].reshape(EXPERTS, CAP))

def reference(hidden_in, doc_ids, routes, out_grad, norm1_gain, q_weight, k_weight, v_weight, o_weight, q_gain, k_gain, norm2_gain, router_weight, gate_weight, up_weight, down_weight):
    groups = doc_ids.shape[0]
    route_rows = routes.reshape(groups, TOK_DEV, TOPK)
    slot_ids, owners = jax.vmap(slot_tables)(route_rows)
    kept_mask = slot_ids < EXPERTS * CAP
    group_index = jnp.arange(groups, dtype=jnp.int32)[:, None, None]
    flat_index = jnp.where(kept_mask, slot_ids // CAP * (groups * CAP) + group_index * CAP + slot_ids % CAP, EXPERTS * groups * CAP).astype(jnp.int32)
    pick_mask = (route_rows[..., None] == jnp.arange(EXPERTS, dtype=jnp.int32)).astype(jnp.float32)
    attend_step = jax.checkpoint(attend_group)
    expert_step = jax.checkpoint(expert_rows)
    owner_rows = jnp.transpose(owners, (1, 0, 2))

    def forward(inputs, g_one, w_query, w_key, w_value, w_out, q_scale, k_scale, g_two, w_router, w_gate, w_up, w_down):
        grouped = inputs.reshape(groups, TOK_DEV, D)
        after_attn = lax.map(lambda packed: attend_step(packed[0], packed[1], g_one, w_query, w_key, w_value, w_out, q_scale, k_scale), (grouped, doc_ids))
        normed = low(after_attn * rms_scale(after_attn) * g_two)
        logits = low_back(jnp.einsum('gtd,de->gte', normed, w_router, precision=precise))
        chosen = lax.optimization_barrier(jnp.sum(pick_mask * logits[:, :, None, :], -1))
        gates = jax.nn.softmax(chosen, -1)
        padded = jnp.concatenate([normed, jnp.zeros((groups, 1, D), jnp.float32)], 1)
        expert_out = lax.map(lambda packed: expert_step(padded, packed[0], packed[1], packed[2], packed[3]), (w_gate, w_up, w_down, owner_rows))
        flat_out = jnp.concatenate([expert_out.reshape(EXPERTS * groups * CAP, D), jnp.zeros((1, D), jnp.float32)], 0)
        mixture = jnp.zeros((groups, TOK_DEV, D), jnp.float32)
        for rank_k in range(TOPK):
            mixture = mixture + gates[:, :, rank_k, None] * jnp.take(flat_out, flat_index[:, :, rank_k], axis=0)
        return (after_attn + mixture).reshape(groups * TOK_DEV, D)
    primals = (hidden_in.astype(jnp.float32), norm1_gain, q_weight.astype(jnp.float32), k_weight.astype(jnp.float32), v_weight.astype(jnp.float32), o_weight.astype(jnp.float32), q_gain, k_gain, norm2_gain, router_weight.astype(jnp.float32), gate_weight.astype(jnp.float32), up_weight.astype(jnp.float32), down_weight.astype(jnp.float32))
    result, pullback = jax.vjp(forward, *primals)
    grads = pullback(out_grad.astype(jnp.float32))
    return (result.astype(jnp.bfloat16), grads[0], grads[1], grads[2], grads[3], grads[4], grads[5], grads[6], grads[7], grads[8], grads[9], grads[10], grads[11], grads[12])
```

```python
import jax
import jax.numpy as jnp
from jax import lax
from jax.sharding import PartitionSpec as P

epsilon = 1e-06
rope_base = 10000.0
masked_score = -1e30


def rms_scale(values):
    return lax.rsqrt(jnp.mean(values * values, axis=-1, keepdims=True) + epsilon)


def rotary(positions, head_size):
    half_size = head_size // 2
    freqs = rope_base ** (-2.0 * jnp.arange(half_size, dtype=jnp.float32) / head_size)
    angles = jnp.arange(positions, dtype=jnp.float32)[:, None] * freqs[None, :]
    cosine = jnp.cos(angles)
    sine = jnp.sin(angles)
    return (jnp.concatenate([cosine, cosine], -1), jnp.concatenate([sine, sine], -1))


def prep_heads(raw, gain, factor, cosine, sine, heads):
    shaped = raw.reshape(raw.shape[0], heads, -1)
    normed = shaped * rms_scale(shaped) * gain
    half_size = normed.shape[-1] // 2
    turned = jnp.concatenate([-normed[..., half_size:], normed[..., :half_size]], -1)
    return (normed * cosine[:, None, :] + turned * sine[:, None, :]) * factor


def slot_tables(route_rows, all_experts, capacity):
    num_tokens, num_picks = route_rows.shape
    flat_routes = route_rows.reshape(-1)
    onehot = (flat_routes[:, None] == jnp.arange(all_experts, dtype=jnp.int32)[None, :]).astype(
        jnp.int32
    )
    before = jnp.cumsum(onehot, axis=0) - onehot
    placed = jnp.sum(before * onehot, axis=1)
    slot_ids = jnp.where(placed < capacity, flat_routes * capacity + placed, all_experts * capacity)
    pair_ids = jnp.arange(num_tokens * num_picks, dtype=jnp.int32)
    pair_of = (
        jnp.full((all_experts * capacity + 1,), num_tokens * num_picks, jnp.int32)
        .at[slot_ids]
        .set(pair_ids)
    )
    return (slot_ids.reshape(num_tokens, num_picks), pair_of[:-1])


def on_device(
    hidden_in,
    doc_ids,
    routes,
    out_grad,
    norm1_gain,
    q_weight,
    k_weight,
    v_weight,
    o_weight,
    q_gain,
    k_gain,
    norm2_gain,
    router_weight,
    gate_weight,
    up_weight,
    down_weight,
):
    num_tokens, model_width = hidden_in.shape
    num_picks = routes.shape[1]
    head_size = q_gain.shape[0]
    local_heads = q_weight.shape[1] // head_size
    local_experts = gate_weight.shape[0]
    ffn_local = gate_weight.shape[2]
    expert_ranks = lax.axis_size("expert")
    tensor_ranks = lax.axis_size("tensor")
    all_experts = local_experts * expert_ranks
    capacity = tensor_ranks * (
        (9 * num_tokens * num_picks + 8 * all_experts * tensor_ranks - 1)
        // (8 * all_experts * tensor_ranks)
    )
    doc_row = doc_ids[0]
    cosine, sine = rotary(num_tokens, head_size)
    zero_row = jnp.zeros((1, model_width), jnp.bfloat16)
    inputs = hidden_in.astype(jnp.float32)
    scale_one = rms_scale(inputs)
    unit_one = inputs * scale_one
    normed_one = (unit_one * norm1_gain).astype(jnp.bfloat16)
    q_raw = jnp.dot(normed_one, q_weight, preferred_element_type=jnp.float32)
    k_raw = jnp.dot(normed_one, k_weight, preferred_element_type=jnp.float32)
    v_raw = jnp.dot(normed_one, v_weight, preferred_element_type=jnp.float32)

    def shape_heads(q_in, k_in, q_scale, k_scale):
        return (
            prep_heads(q_in, q_scale, head_size ** (-0.5), cosine, sine, local_heads),
            prep_heads(k_in, k_scale, 1.0, cosine, sine, local_heads),
        )

    head_vals, head_back = jax.vjp(shape_heads, q_raw, k_raw, q_gain, k_gain)
    queries = head_vals[0].astype(jnp.bfloat16)
    keys = head_vals[1].astype(jnp.bfloat16)
    values = v_raw.astype(jnp.bfloat16).reshape(num_tokens, local_heads, head_size)

    def block_scores():
        scores = jnp.einsum("qhd,khd->hqk", queries, keys, preferred_element_type=jnp.float32)
        return (
            jnp.where((doc_row[:, None] == doc_row[None, :])[None], scores, masked_score),
            queries,
        )

    scores, query_blk = block_scores()
    peak = jnp.max(scores, -1, keepdims=True)
    log_total = peak + jnp.log(jnp.sum(jnp.exp(scores - peak), -1, keepdims=True))
    weights = jnp.exp(scores - log_total).astype(jnp.bfloat16)
    block_outs = jnp.einsum("hqk,khd->qhd", weights, values, preferred_element_type=jnp.float32)
    attn_out = block_outs.reshape(num_tokens, local_heads * head_size).astype(jnp.bfloat16)
    attn_part = lax.dot_general(
        attn_out, o_weight, (((1,), (1,)), ((), ())), preferred_element_type=jnp.float32
    )
    attn_full = lax.psum(attn_part, "tensor")
    after_attn = inputs + attn_full
    scale_two = rms_scale(after_attn)
    unit_two = after_attn * scale_two
    normed_two = (unit_two * norm2_gain).astype(jnp.bfloat16)
    logits = jnp.dot(normed_two, router_weight, preferred_element_type=jnp.float32)
    pick_mask = routes[:, :, None] == jnp.arange(all_experts, dtype=jnp.int32)[None, None, :]
    chosen = jnp.sum(jnp.where(pick_mask, logits[:, None, :], 0.0), -1)
    gates = jax.nn.softmax(chosen, -1)
    slot_ids, pair_of = slot_tables(routes, all_experts, capacity)
    owners = pair_of // num_picks
    padded_rows = jnp.concatenate([normed_two, zero_row], 0)
    send_buf = jnp.take(padded_rows, owners, axis=0).reshape(
        expert_ranks, local_experts, capacity, model_width
    )
    slot_rows = lax.all_to_all(send_buf, "expert", split_axis=0, concat_axis=0, tiled=True)
    gate_up = jnp.concatenate([gate_weight, up_weight], 2)
    joint_pre = jnp.einsum("secd,edf->secf", slot_rows, gate_up, preferred_element_type=jnp.float32)
    gate_pre = joint_pre[..., :ffn_local]
    up_pre = joint_pre[..., ffn_local:]
    silu_gate = jax.nn.silu(gate_pre)
    hidden = (silu_gate * up_pre).astype(jnp.bfloat16)
    partial_out = jnp.einsum(
        "secf,efd->secd", hidden, down_weight, preferred_element_type=jnp.float32
    ).astype(jnp.bfloat16)
    out_grads = out_grad.astype(jnp.float32)
    mixture = jnp.zeros((num_tokens, model_width), jnp.float32)
    gate_dots = []
    returned = lax.all_to_all(
        partial_out, "expert", split_axis=0, concat_axis=0, tiled=True
    ).reshape(all_experts * capacity, model_width)
    returned = jnp.concatenate([returned, zero_row], 0)
    for rank_k in range(num_picks):
        picked = jnp.take(returned, slot_ids[:, rank_k], axis=0)
        mixture = mixture + gates[:, rank_k, None] * picked
        gate_dots.append(jnp.sum(out_grads * picked, -1))
    moe_full = lax.psum(mixture.astype(jnp.bfloat16), "tensor").astype(jnp.float32)
    output = (after_attn + moe_full).astype(jnp.bfloat16)
    dgate_part = jnp.stack(gate_dots, -1)
    padded_gates = jnp.concatenate([gates.reshape(-1), jnp.zeros((1,), jnp.float32)], 0)
    padded_grads = jnp.concatenate([out_grads, jnp.zeros((1, model_width), jnp.float32)], 0)
    slot_gate = jnp.take(padded_gates, pair_of, axis=0)
    grad_buf = (slot_gate[:, None] * jnp.take(padded_grads, owners, axis=0)).astype(jnp.bfloat16)
    grads_in = lax.all_to_all(
        grad_buf.reshape(expert_ranks, local_experts, capacity, model_width),
        "expert",
        split_axis=0,
        concat_axis=0,
        tiled=True,
    )
    dhidden = jnp.einsum(
        "secd,efd->secf", grads_in, down_weight, preferred_element_type=jnp.float32
    )
    down_grad = jnp.einsum("secf,secd->efd", hidden, grads_in, preferred_element_type=jnp.float32)
    sig_gate = jax.nn.sigmoid(gate_pre)
    dgate_pre = dhidden * up_pre * (sig_gate * (1.0 + gate_pre * (1.0 - sig_gate)))
    dup_pre = dhidden * silu_gate
    djoint = jnp.concatenate([dgate_pre, dup_pre], -1).astype(jnp.bfloat16)
    joint_grad = jnp.einsum("secd,secf->edf", slot_rows, djoint, preferred_element_type=jnp.float32)
    gate_grad = joint_grad[..., :ffn_local]
    up_grad = joint_grad[..., ffn_local:]
    dslot_in = jnp.einsum(
        "secf,edf->secd", djoint, gate_up, preferred_element_type=jnp.float32
    ).astype(jnp.bfloat16)
    dnormed_part = jnp.zeros((num_tokens, model_width), jnp.float32)
    came_back = lax.all_to_all(dslot_in, "expert", split_axis=0, concat_axis=0, tiled=True).reshape(
        all_experts * capacity, model_width
    )
    came_back = jnp.concatenate([came_back, zero_row], 0)
    for rank_k in range(num_picks):
        dnormed_part = dnormed_part + jnp.take(came_back, slot_ids[:, rank_k], axis=0)
    dnormed_exp, dgate_all = lax.psum((dnormed_part, dgate_part), "tensor")
    dsel = gates * (dgate_all - jnp.sum(gates * dgate_all, -1, keepdims=True))
    dlogits = jnp.sum(jnp.where(pick_mask, dsel[:, :, None], 0.0), 1).astype(jnp.bfloat16)
    router_grad = lax.dot_general(
        normed_two, dlogits, (((0,), (0,)), ((), ())), preferred_element_type=jnp.float32
    )
    dnormed_two = dnormed_exp + lax.dot_general(
        dlogits, router_weight, (((1,), (1,)), ((), ())), preferred_element_type=jnp.float32
    )
    norm2_grad = jnp.sum(dnormed_two * unit_two, 0)
    weighted_two = dnormed_two * norm2_gain
    dafter = out_grads + scale_two * (
        weighted_two - unit_two * jnp.mean(weighted_two * unit_two, -1, keepdims=True)
    )
    dattn = dafter.astype(jnp.bfloat16)
    o_grad = lax.dot_general(
        dattn, attn_out, (((0,), (0,)), ((), ())), preferred_element_type=jnp.float32
    )
    dattn_out = (
        jnp.dot(dattn, o_weight, preferred_element_type=jnp.float32)
        .astype(jnp.bfloat16)
        .reshape(num_tokens, local_heads, head_size)
    )
    scores, query_blk = block_scores()
    probs = jnp.exp(scores - log_total)
    dprobs = jnp.einsum("qhd,khd->hqk", dattn_out, values, preferred_element_type=jnp.float32)
    dscores = (probs * (dprobs - jnp.sum(probs * dprobs, -1, keepdims=True))).astype(jnp.bfloat16)
    dquery_blocks = jnp.einsum("hqk,khd->qhd", dscores, keys, preferred_element_type=jnp.float32)
    dkey = jnp.einsum("hqk,qhd->khd", dscores, query_blk, preferred_element_type=jnp.float32)
    dvalue = jnp.einsum(
        "hqk,qhd->khd", probs.astype(jnp.bfloat16), dattn_out, preferred_element_type=jnp.float32
    )
    dq_raw, dk_raw, q_gain_part, k_gain_part = head_back((dquery_blocks, dkey))
    dq_low = dq_raw.astype(jnp.bfloat16)
    dk_low = dk_raw.astype(jnp.bfloat16)
    dv_low = dvalue.reshape(num_tokens, local_heads * head_size).astype(jnp.bfloat16)
    contract_rows = (((0,), (0,)), ((), ()))
    contract_cols = (((1,), (1,)), ((), ()))
    q_grad = lax.dot_general(normed_one, dq_low, contract_rows, preferred_element_type=jnp.float32)
    k_grad = lax.dot_general(normed_one, dk_low, contract_rows, preferred_element_type=jnp.float32)
    v_grad = lax.dot_general(normed_one, dv_low, contract_rows, preferred_element_type=jnp.float32)
    dnormed_one = lax.dot_general(
        dq_low, q_weight, contract_cols, preferred_element_type=jnp.float32
    )
    dnormed_one = dnormed_one + lax.dot_general(
        dk_low, k_weight, contract_cols, preferred_element_type=jnp.float32
    )
    dnormed_one = dnormed_one + lax.dot_general(
        dv_low, v_weight, contract_cols, preferred_element_type=jnp.float32
    )
    dnormed_full, q_gain_sum, k_gain_sum = (
        lax.psum(dnormed_one.astype(jnp.bfloat16), "tensor").astype(jnp.float32),
        lax.psum(q_gain_part.astype(jnp.bfloat16), "tensor").astype(jnp.float32),
        lax.psum(k_gain_part.astype(jnp.bfloat16), "tensor").astype(jnp.float32),
    )
    norm1_grad = jnp.sum(dnormed_full * unit_one, 0)
    weighted_one = dnormed_full * norm1_gain
    input_grad = dafter + scale_one * (
        weighted_one - unit_one * jnp.mean(weighted_one * unit_one, -1, keepdims=True)
    )
    reduced = (
        lax.psum_scatter(
            q_grad.astype(jnp.bfloat16), "expert", scatter_dimension=0, tiled=True
        ).astype(jnp.float32),
        lax.psum_scatter(
            k_grad.astype(jnp.bfloat16), "expert", scatter_dimension=0, tiled=True
        ).astype(jnp.float32),
        lax.psum_scatter(
            v_grad.astype(jnp.bfloat16), "expert", scatter_dimension=0, tiled=True
        ).astype(jnp.float32),
        lax.psum_scatter(
            o_grad.astype(jnp.bfloat16), "expert", scatter_dimension=0, tiled=True
        ).astype(jnp.float32),
        lax.psum_scatter(
            router_grad.astype(jnp.bfloat16), "expert", scatter_dimension=0, tiled=True
        ).astype(jnp.float32),
        lax.psum_scatter(
            norm1_grad.astype(jnp.bfloat16), "expert", scatter_dimension=0, tiled=True
        ).astype(jnp.float32),
        lax.psum_scatter(
            norm2_grad.astype(jnp.bfloat16), "expert", scatter_dimension=0, tiled=True
        ).astype(jnp.float32),
        lax.psum_scatter(
            q_gain_sum.astype(jnp.bfloat16), "expert", scatter_dimension=0, tiled=True
        ).astype(jnp.float32),
        lax.psum_scatter(
            k_gain_sum.astype(jnp.bfloat16), "expert", scatter_dimension=0, tiled=True
        ).astype(jnp.float32),
    )
    return (
        output,
        input_grad,
        reduced[5],
        reduced[0],
        reduced[1],
        reduced[2],
        reduced[3],
        reduced[7],
        reduced[8],
        reduced[6],
        reduced[4],
        gate_grad,
        up_grad,
        down_grad,
    )


def product(left, right, left_dim, right_dim):
    return lax.dot_general(
        left, right, (((left_dim,), (right_dim,)), ((), ())), preferred_element_type=jnp.float32
    )


def swap(value, axis, bit):
    ranks = lax.axis_size(axis)
    return lax.ppermute(value, axis, [(rank, rank ^ bit) for rank in range(ranks)])


def low_sum(left, right):
    return (left.astype(jnp.float32) + right.astype(jnp.float32)).astype(jnp.bfloat16)


def gather_near(own, first_bits):
    (axis_a, bit_a), (axis_b, bit_b) = first_bits
    near_a = swap(own, axis_a, bit_a)
    near_b = swap(own, axis_b, bit_b)
    near_ab = swap(near_a, axis_b, bit_b)
    chips = [own, near_a, near_b, near_ab]
    return chips + [swap(shard, "tensor", 1) for shard in chips]


def scatter_near(blocks, first_bits):
    (axis_a, bit_a), (axis_b, bit_b) = first_bits
    half = blocks.shape[0] // 2
    chips = low_sum(blocks[:half], swap(blocks[half:], "tensor", 1))
    half = half // 2
    pair = low_sum(chips[:half], swap(chips[half:], axis_b, bit_b))
    half = half // 2
    return low_sum(pair[:half], swap(pair[half:], axis_a, bit_a))


def scatter_rows(shards):
    first = low_sum(shards[0], swap(shards[1], "tensor", 1))
    second = low_sum(shards[2], swap(shards[3], "tensor", 1))
    return first.astype(jnp.float32) + swap(second, "tensor", 2).astype(jnp.float32)


def gather_rows(own):
    across = swap(own, "tensor", 2)
    return [own, swap(own, "tensor", 1), across, swap(across, "tensor", 1)]


def total_over_all(value):
    for bit in (1, 2):
        value = value + swap(value, "tensor", bit)
    for bit in (1, 2, 4):
        value = value + swap(value, "expert", bit)
    return value


def dense_on_device(
    hidden_in,
    doc_ids,
    routes,
    out_grad,
    norm1_gain,
    q_weight,
    k_weight,
    v_weight,
    o_weight,
    q_gain,
    k_gain,
    norm2_gain,
    router_weight,
    gate_weight,
    up_weight,
    down_weight,
):
    num_tokens, model_width = hidden_in.shape
    num_picks = routes.shape[1]
    head_size = q_gain.shape[0]
    local_heads = q_weight.shape[1] // head_size
    local_experts, _, ffn_local = gate_weight.shape
    expert_ranks = lax.axis_size("expert")
    tensor_ranks = lax.axis_size("tensor")
    all_experts = local_experts * expert_ranks
    capacity = tensor_ranks * (
        (9 * num_tokens * num_picks + 8 * all_experts * tensor_ranks - 1)
        // (8 * all_experts * tensor_ranks)
    )
    expert_rank = lax.axis_index("expert")
    tensor_rank = lax.axis_index("tensor")
    own_tokens = num_tokens // tensor_ranks
    extra = 128
    order = [tensor_rank ^ step for step in range(tensor_ranks)]

    def own_rows(value):
        return lax.dynamic_slice_in_dim(value, tensor_rank * own_tokens, own_tokens, 0)

    def near_rows(value):
        return jnp.concatenate(
            [lax.dynamic_slice_in_dim(value, rank * own_tokens, own_tokens, 0) for rank in order], 0
        )

    def true_rows(shards, kind):
        whole = jnp.zeros((num_tokens, model_width), kind)
        for rank, shard in zip(order, shards):
            whole = lax.dynamic_update_slice_in_dim(
                whole, shard.astype(kind), rank * own_tokens, 0
            )
        return whole

    expert_ids = jnp.arange(all_experts, dtype=jnp.int32)
    routed = jnp.any(routes[:, :, None] == expert_ids[None, None, :], 1)
    routed_low = routed.astype(jnp.bfloat16)
    earlier = (
        jnp.arange(num_tokens, dtype=jnp.int32)[None, :]
        < jnp.arange(num_tokens, dtype=jnp.int32)[:, None]
    ).astype(jnp.bfloat16)
    places = product(earlier, routed_low, 1, 0)
    kept = jnp.where(routed & (places < capacity), 1.0, 0.0)
    own_routed = own_rows(routed_low) > 0
    own_kept = own_rows(kept)

    bits = {0: (("expert", 1), ("tensor", 2)), 1: (("tensor", 2), ("expert", 1))}
    groups = expert_ranks // 2

    def gather_all(own):
        parts = [own if step == 0 else swap(own, "expert", 2 * step) for step in range(groups)]
        return [gather_near(part, bits[step % 2]) for step, part in enumerate(parts)]

    def scatter_all(blocks):
        sums = [scatter_near(block, bits[step % 2]) for step, block in enumerate(blocks)]
        total = sums[0].astype(jnp.float32)
        for step in range(1, groups):
            total = total + swap(sums[step], "expert", 2 * step).astype(jnp.float32)
        return total

    own_grads = own_rows(out_grad)
    grad_groups = [jnp.concatenate(parts, 0) for parts in gather_all(own_grads)]
    down_joint = down_weight.reshape(local_experts * ffn_local, model_width)

    rows_low = near_rows(hidden_in)
    doc_row = near_rows(doc_ids[0])
    local_index = jnp.arange(num_tokens, dtype=jnp.int32)
    positions = ((local_index // own_tokens) ^ tensor_rank) * own_tokens + local_index % own_tokens
    half_size = head_size // 2
    freqs = rope_base ** (-2.0 * jnp.arange(half_size, dtype=jnp.float32) / head_size)
    angles = positions.astype(jnp.float32)[:, None] * freqs[None, :]
    cosine = jnp.cos(angles)
    sine = jnp.sin(angles)
    cosine = jnp.concatenate([cosine, cosine], -1)
    sine = jnp.concatenate([sine, sine], -1)

    inputs = rows_low.astype(jnp.float32)
    normed_one = (inputs * rms_scale(inputs) * norm1_gain).astype(jnp.bfloat16)
    q_raw = product(normed_one, q_weight, 1, 0)
    k_raw = product(normed_one, k_weight, 1, 0)
    v_raw = product(normed_one, v_weight, 1, 0)

    def shape_heads(q_in, k_in, q_scale, k_scale):
        return (
            prep_heads(q_in, q_scale, head_size ** (-0.5), cosine, sine, local_heads),
            prep_heads(k_in, k_scale, 1.0, cosine, sine, local_heads),
        )

    head_vals, head_back = jax.vjp(shape_heads, q_raw, k_raw, q_gain, k_gain)
    queries = head_vals[0].astype(jnp.bfloat16)
    keys = head_vals[1].astype(jnp.bfloat16)
    values = v_raw.astype(jnp.bfloat16).reshape(num_tokens, local_heads, head_size)
    same_doc = (doc_row[:, None] == doc_row[None, :])[None]
    scores = jnp.einsum("qhd,khd->hqk", queries, keys, preferred_element_type=jnp.float32)
    scores = jnp.where(same_doc, scores, masked_score)
    peak = jnp.max(scores, -1, keepdims=True)
    log_total = peak + jnp.log(jnp.sum(jnp.exp(scores - peak), -1, keepdims=True))
    probs = jnp.exp(scores - log_total)
    probs_low = probs.astype(jnp.bfloat16)
    block_outs = jnp.einsum("hqk,khd->qhd", probs_low, values, preferred_element_type=jnp.float32)
    attn_out = block_outs.reshape(num_tokens, local_heads * head_size).astype(jnp.bfloat16)
    attn_part = product(attn_out, o_weight, 1, 1).astype(jnp.bfloat16)

    attn_own = scatter_rows(jnp.split(attn_part, tensor_ranks, 0))
    own_inputs = own_rows(hidden_in).astype(jnp.float32)
    after_attn = own_inputs + attn_own
    scale_two = rms_scale(after_attn)
    unit_two = after_attn * scale_two
    normed_two = (unit_two * norm2_gain).astype(jnp.bfloat16)
    logits = product(normed_two, router_weight, 1, 0)
    top_logit = jnp.max(jnp.where(own_routed, logits, masked_score), -1, keepdims=True)
    raised = jnp.where(own_routed, jnp.exp(jnp.where(own_routed, logits - top_logit, 0.0)), 0.0)
    gates = raised / jnp.sum(raised, -1, keepdims=True)
    kept_gates = gates * own_kept
    gates_high = kept_gates.astype(jnp.bfloat16)
    gates_rest = (kept_gates - gates_high.astype(jnp.float32)).astype(jnp.bfloat16)
    spare = jnp.zeros((own_tokens, extra - 2 * all_experts), jnp.bfloat16)
    sent_rows = jnp.concatenate([normed_two, gates_high, gates_rest, spare], 1)

    joint_weight = jnp.concatenate(
        [gate_weight[index] for index in range(local_experts)]
        + [up_weight[index] for index in range(local_experts)],
        1,
    )
    width = local_experts * ffn_local
    chosen_one = [
        (expert_ids == expert_rank * local_experts + index).astype(jnp.float32)
        for index in range(local_experts)
    ]
    row_groups = [jnp.concatenate(parts, 0) for parts in gather_all(sent_rows)]
    hidden_groups = []
    djoint_groups = []
    back_groups = []
    for rows_ext, grads in zip(row_groups, grad_groups):
        rows = rows_ext[:, :model_width]
        tail = rows_ext[:, model_width:].astype(jnp.float32)
        row_gates = tail[:, :all_experts] + tail[:, all_experts : 2 * all_experts]
        dhidden = product(grads, down_joint, 1, 1)
        joint = product(rows, joint_weight, 1, 0)
        gate_pre = joint[:, :width]
        up_pre = joint[:, width:]
        sig_gate = jax.nn.sigmoid(gate_pre)
        silu_gate = gate_pre * sig_gate
        hidden = silu_gate * up_pre
        gate_cols = []
        dgates = jnp.zeros((rows.shape[0], all_experts), jnp.float32)
        for index in range(local_experts):
            cols = slice(index * ffn_local, (index + 1) * ffn_local)
            picked = jnp.sum(row_gates * chosen_one[index], -1, keepdims=True)
            gate_cols.append(jnp.broadcast_to(picked, (rows.shape[0], ffn_local)))
            dots = jnp.sum(hidden[:, cols] * dhidden[:, cols], -1, keepdims=True)
            dgates = dgates + dots * chosen_one[index]
        gate_wide = jnp.concatenate(gate_cols, 1)
        hidden_groups.append((hidden * gate_wide).astype(jnp.bfloat16))
        dscaled = dhidden * gate_wide
        dgate_pre = dscaled * up_pre * (sig_gate * (1.0 + gate_pre * (1.0 - sig_gate)))
        djoint = jnp.concatenate([dgate_pre, dscaled * silu_gate], 1).astype(jnp.bfloat16)
        djoint_groups.append(djoint)
        drows = product(djoint, joint_weight, 1, 1).astype(jnp.bfloat16)
        gap = jnp.zeros((rows.shape[0], extra - all_experts), jnp.bfloat16)
        back_groups.append(jnp.concatenate([drows, dgates.astype(jnp.bfloat16), gap], 1))

    back_own = scatter_all(back_groups)
    mix_groups = [product(hidden, down_joint, 1, 0).astype(jnp.bfloat16) for hidden in hidden_groups]
    mixture = scatter_all(mix_groups)
    hidden_all = jnp.concatenate(hidden_groups, 0)
    djoint_all = jnp.concatenate(djoint_groups, 0)
    grads_all = jnp.concatenate(grad_groups, 0)
    rows_all = jnp.concatenate([rows_ext[:, :model_width] for rows_ext in row_groups], 0)
    down_grad = product(hidden_all, grads_all, 0, 0).reshape(down_weight.shape)
    joint_grad = product(rows_all, djoint_all, 0, 0)
    gate_grad = jnp.stack(
        [joint_grad[:, index * ffn_local : (index + 1) * ffn_local] for index in range(local_experts)]
    )
    up_grad = jnp.stack(
        [
            joint_grad[:, width + index * ffn_local : width + (index + 1) * ffn_local]
            for index in range(local_experts)
        ]
    )
    output = true_rows(gather_rows((after_attn + mixture).astype(jnp.bfloat16)), jnp.bfloat16)

    dgate_own = back_own[:, model_width : model_width + all_experts] * own_kept
    dsel = gates * (dgate_own - jnp.sum(gates * dgate_own, -1, keepdims=True))
    dlogits = dsel.astype(jnp.bfloat16)
    router_part = product(normed_two, dlogits, 0, 0)
    dnormed_two = back_own[:, :model_width] + product(dlogits, router_weight, 1, 1)
    norm2_part = jnp.sum(dnormed_two * unit_two, 0)
    weighted_two = dnormed_two * norm2_gain
    dafter = own_grads.astype(jnp.float32) + scale_two * (
        weighted_two - unit_two * jnp.mean(weighted_two * unit_two, -1, keepdims=True)
    )
    dattn = jnp.concatenate(gather_rows(dafter.astype(jnp.bfloat16)), 0)

    grad_rows = model_width // expert_ranks
    steps = list(range(0, expert_ranks, 2)) + list(range(1, expert_ranks, 2))

    def near_cols(value):
        return jnp.concatenate(
            [
                lax.dynamic_slice_in_dim(value, (expert_rank ^ step) * grad_rows, grad_rows, 1)
                for step in steps
            ],
            1,
        )

    def scatter_grad(partial):
        half = partial.shape[0] // 2
        near = low_sum(partial[:half], swap(partial[half:], "expert", 1))
        parts = jnp.split(near, groups, 0)
        total = parts[0].astype(jnp.float32)
        for step in range(1, groups):
            total = total + swap(parts[step], "expert", 2 * step).astype(jnp.float32)
        return total

    o_grad = scatter_grad(product(near_cols(dattn), attn_out, 0, 0).astype(jnp.bfloat16))

    dattn_out = (
        product(dattn, o_weight, 1, 0)
        .astype(jnp.bfloat16)
        .reshape(num_tokens, local_heads, head_size)
    )
    dprobs = jnp.einsum("qhd,khd->hqk", dattn_out, values, preferred_element_type=jnp.float32)
    dscores = (probs * (dprobs - jnp.sum(probs * dprobs, -1, keepdims=True))).astype(jnp.bfloat16)
    dquery = jnp.einsum("hqk,khd->qhd", dscores, keys, preferred_element_type=jnp.float32)
    dkey = jnp.einsum("hqk,qhd->khd", dscores, queries, preferred_element_type=jnp.float32)
    dvalue = jnp.einsum("hqk,qhd->khd", probs_low, dattn_out, preferred_element_type=jnp.float32)
    dq_raw, dk_raw, q_gain_part, k_gain_part = head_back((dquery, dkey))
    dq_low = dq_raw.astype(jnp.bfloat16)
    dk_low = dk_raw.astype(jnp.bfloat16)
    dv_low = dvalue.reshape(num_tokens, local_heads * head_size).astype(jnp.bfloat16)
    normed_cols = near_cols(normed_one)
    v_grad = scatter_grad(product(normed_cols, dv_low, 0, 0).astype(jnp.bfloat16))
    k_grad = scatter_grad(product(normed_cols, dk_low, 0, 0).astype(jnp.bfloat16))
    q_grad = scatter_grad(product(normed_cols, dq_low, 0, 0).astype(jnp.bfloat16))
    dnormed_one = product(dq_low, q_weight, 1, 1)
    dnormed_one = dnormed_one + product(dk_low, k_weight, 1, 1)
    dnormed_one = dnormed_one + product(dv_low, v_weight, 1, 1)
    dnormed_own = scatter_rows(jnp.split(dnormed_one.astype(jnp.bfloat16), tensor_ranks, 0))
    scale_one = rms_scale(own_inputs)
    unit_one = own_inputs * scale_one
    norm1_part = jnp.sum(dnormed_own * unit_one, 0)
    weighted_one = dnormed_own * norm1_gain
    input_own = dafter + scale_one * (
        weighted_one - unit_one * jnp.mean(weighted_one * unit_one, -1, keepdims=True)
    )
    input_grad = true_rows(gather_rows(input_own.astype(jnp.bfloat16)), jnp.float32)

    def own_part(value):
        size = value.shape[0] // expert_ranks
        return lax.dynamic_slice_in_dim(value, expert_rank * size, size, 0)

    first_sums = total_over_all(
        jnp.concatenate([router_part.reshape(-1, 128), norm2_part.reshape(-1, 128)], 0)
    )
    last_sums = total_over_all(
        jnp.concatenate(
            [norm1_part.reshape(-1, 128), q_gain_part[None, :], k_gain_part[None, :]], 0
        )
    )
    router_rows = router_part.size // 128
    norm_rows = model_width // 128
    router_grad = own_part(first_sums[:router_rows].reshape(router_part.shape))
    norm2_grad = own_part(first_sums[router_rows:].reshape(-1))
    norm1_grad = own_part(last_sums[:norm_rows].reshape(-1))
    q_gain_grad = own_part(last_sums[norm_rows])
    k_gain_grad = own_part(last_sums[norm_rows + 1])
    return (
        output,
        input_grad,
        norm1_grad,
        q_grad,
        k_grad,
        v_grad,
        o_grad,
        q_gain_grad,
        k_gain_grad,
        norm2_grad,
        router_grad,
        gate_grad,
        up_grad,
        down_grad,
    )


def solution(mesh):
    dense = mesh.shape["expert"] == 8 and mesh.shape["tensor"] == 4
    return jax.shard_map(
        dense_on_device if dense else on_device,
        mesh=mesh,
        in_specs=(
            P("expert", None),
            P("expert", None),
            P("expert", None),
            P("expert", None),
            P(),
            P(None, "tensor"),
            P(None, "tensor"),
            P(None, "tensor"),
            P(None, "tensor"),
            P(),
            P(),
            P(),
            P(),
            P("expert", None, "tensor"),
            P("expert", None, "tensor"),
            P("expert", "tensor", None),
        ),
        out_specs=(
            P("expert", None),
            P("expert", None),
            P("expert"),
            P("expert", "tensor"),
            P("expert", "tensor"),
            P("expert", "tensor"),
            P("expert", "tensor"),
            P("expert"),
            P("expert"),
            P("expert"),
            P("expert", None),
            P("expert", None, "tensor"),
            P("expert", None, "tensor"),
            P("expert", "tensor", None),
        ),
        check_vma=False,
    )
```
